32 devices in a mesh: row: 4 (over x, core), col: 4 (over z), depth: 2 (over y).
Axes of the slice: x: 2, y: 2, z: 4, core: 2. Of those that a mesh axis runs over, the one named last changes fastest.
Arguments:
- candidates: bfloat16 [4096, 512], P('row', ('col', 'depth')), may hold values from -6 to 6
- references: bfloat16 [16384, 512], P(('col', 'depth'), 'row'), may hold values from -6 to 6
- rates: float32 [16384], P(('col', 'depth')), may hold values from 0.15 to 1.5
Outputs:
- kernel: float32 [4096, 16384], P('row', ('col', 'depth'))
The draws below stay inside these ranges and needn't reach their ends.
All inputs are finite; a program needn't handle non-finite values.
Results may differ from the reference program's by a relative error of at most 0.0003.
Values may be sent and summed in bfloat16 or wider, within the bound.
No kernel may reach another device: no remote copies, remote signals or barrier semaphores. Data moves between devices by JAX's collectives and lax.ppermute only.
A program may use at most 64 MiB of HBM per device.

```python
import math
import jax
import jax.numpy as jnp
from jax import lax

D = 512
CAND_ROWS = 1024
CAND_TOTAL = 4096
REF_TOTAL = 16384
N_ROW = 4


def shard_levels(stream_key, extent, shards, low, top_value):
    loudness = 1.0
    for position, parts in shards:
        steps = jax.random.uniform(jax.random.fold_in(jax.random.fold_in(stream_key, 6), position), (parts,), jnp.float32, low / len(shards), top_value / len(shards))
        loudness = loudness * jnp.repeat(jnp.exp(steps), extent[position] // parts).reshape((-1,) + (1,) * (len(extent) - 1 - position))
    return loudness


def normal_values(own_key, extent, deviation, reach, cuts=(), dtype=jnp.bfloat16):
    level = shard_levels(own_key, extent, cuts, -0.22, 0.18) if cuts else 1.0
    result = jax.random.normal(own_key, extent, jnp.float32) * deviation * level
    return jnp.minimum(jnp.maximum(result, -reach), reach).astype(dtype)


def setup_inputs(seed: int = 0) -> dict:
    key_of = jax.random.split(jax.random.key(seed), 4)
    candidates = normal_values(key_of[0], (CAND_TOTAL, D), 1.0, 6.0, ((0, 4), (1, 8)))
    references = normal_values(key_of[1], (REF_TOTAL, D), 1.0, 6.0, ((0, 8), (1, 4)))
    rates = jnp.clip(jnp.exp(math.log(1.5) - 2.3025851 * jax.random.uniform(key_of[2], (REF_TOTAL,), jnp.float32) ** shard_levels(key_of[2], (REF_TOTAL,), ((0, 8),), -0.2, 0.2)), 0.15, 1.5)
    return {"candidates": candidates, "references": references, "rates": rates}


def reference(candidates, references, rates):
    ref_sq = jnp.sum(jnp.square(references.astype(jnp.float32)), axis=1)
    width = candidates.shape[1]
    blocks = candidates.reshape(N_ROW, CAND_ROWS, width)

    def one_block(block):
        cand_sq = jnp.sum(jnp.square(block.astype(jnp.float32)), axis=1)
        gram = lax.dot_general(block, references, (((1,), (1,)), ((), ())), preferred_element_type=jnp.float32)
        distance = cand_sq[:, None] + ref_sq[None, :] - 2.0 * gram
        return jnp.exp(-rates[None, :] * distance / width)

    return lax.map(one_block, blocks).reshape(CAND_TOTAL, REF_TOTAL)
```

```python
import functools

import jax
import jax.numpy as jnp
from jax import lax
from jax.experimental import pallas as pl
from jax.experimental.pallas import tpu as pltpu
from jax.sharding import PartitionSpec as P

LOG2E = 1.4426950408889634


def swap(value, axis, size, bit):
    return lax.ppermute(value, axis, [(i, i ^ bit) for i in range(size)])


def similarity_kernel(place, *refs, n_cand, n_ref, width):
    cands, rows = refs[:n_cand], refs[n_cand : n_cand + n_ref]
    rates, out, panel, lhs, half_sq = refs[n_cand + n_ref :]
    feats = cands[0].shape[0]

    @pl.when(pl.program_id(0) == 0)
    def _():
        for s in range(n_cand):
            panel[pl.ds(pl.multiple_of(place[s] * feats, feats), feats), :] = cands[s][...]
        lhs[...] = panel[...].T
        wide = lhs[...].astype(jnp.float32)
        half_sq[...] = jnp.broadcast_to(
            0.5 * jnp.sum(wide * wide, axis=1, keepdims=True), half_sq.shape
        )

    rhs = [r[...] for r in rows]
    squares = sum(jnp.square(v.astype(jnp.float32)) for v in rhs)
    half_ref = 0.5 * jnp.sum(squares.T, axis=0, keepdims=True)
    scale = rates[...] * (2.0 * LOG2E / width)
    gram = lax.dot_general(
        lhs[...],
        jnp.concatenate(rhs, axis=1),
        (((1,), (1,)), ((), ())),
        preferred_element_type=jnp.float32,
    )
    half_cand = jnp.concatenate([half_sq[...]] * (gram.shape[1] // 128), axis=1)
    out[...] = jnp.exp2((gram - half_cand - half_ref) * scale)


def similarity(cands, rows, rates, place, block):
    feats, m = cands[0].shape
    n, ref_feats = rows[0].shape
    width = feats * len(cands)
    return pl.pallas_call(
        functools.partial(similarity_kernel, n_cand=len(cands), n_ref=len(rows), width=width),
        grid_spec=pltpu.PrefetchScalarGridSpec(
            num_scalar_prefetch=1,
            grid=(n // block,),
            in_specs=[pl.BlockSpec((feats, m), lambda j, _: (0, 0))] * len(cands)
            + [pl.BlockSpec((block, ref_feats), lambda j, _: (j, 0))] * len(rows)
            + [pl.BlockSpec((1, block), lambda j, _: (0, j))],
            out_specs=pl.BlockSpec((m, block), lambda j, _: (0, j)),
            scratch_shapes=[
                pltpu.VMEM((width, m), jnp.bfloat16),
                pltpu.VMEM((m, width), jnp.bfloat16),
                pltpu.VMEM((m, 128), jnp.float32),
            ],
        ),
        out_shape=jax.ShapeDtypeStruct((m, n), jnp.float32),
        compiler_params=pltpu.CompilerParams(vmem_limit_bytes=48 * 2**20),
        name="similarity",
    )(place, *cands, *rows, rates.reshape(1, n))


def per_device(candidates, references, rates, *, n_row, n_col, n_depth):
    far = swap(references, "row", n_row, 2)
    side = swap(references, "row", n_row, 1)
    own = candidates.T
    two = swap(own, "col", n_col, 2)
    one = swap(own, "col", n_col, 1)
    across = [swap(own, "depth", n_depth, 1)]
    two, one, across[0], side = lax.optimization_barrier((two, one, across[0], side))
    three = swap(two, "col", n_col, 1)
    across += [swap(block, "depth", n_depth, 1) for block in (one, two)]
    across.append(swap(three, "depth", n_depth, 1))
    far, across[1], across[2] = lax.optimization_barrier((far, across[1], across[2]))
    rows = [references, side, far, swap(far, "row", n_row, 1)]
    cands = [block for pair in zip((own, one, two, three), across) for block in pair]
    here = lax.axis_index("col") * n_depth + lax.axis_index("depth")
    held = here ^ jnp.arange(len(cands), dtype=jnp.int32)
    share = len(cands) // len(rows)
    place = ((held // share) ^ lax.axis_index("row")) * share + held % share
    return similarity(cands, rows, rates, place.astype(jnp.int32), 256)


def gathered(candidates, references, rates):
    panel = lax.all_gather(candidates, ("col", "depth"), axis=1, tiled=True)
    ref_whole = lax.all_gather(references, "row", axis=1, tiled=True)
    return similarity([panel.T], [ref_whole], rates, jnp.zeros((1,), jnp.int32), 256)


def solution(mesh):
    sizes = mesh.shape
    placed = (P("row", ("col", "depth")), P(("col", "depth"), "row"), P(("col", "depth")))
    small = sizes["row"] == 4 and sizes["col"] == 4 and sizes["depth"] == 2
    body = gathered
    if small:
        body = functools.partial(
            per_device, n_row=sizes["row"], n_col=sizes["col"], n_depth=sizes["depth"]
        )
    return jax.shard_map(
        body,
        mesh=mesh,
        in_specs=placed,
        out_specs=P("row", ("col", "depth")),
        check_vma=False,
    )
```

```python
import functools

import jax
import jax.numpy as jnp
from jax import lax
from jax.experimental import pallas as pl
from jax.experimental.pallas import tpu as pltpu
from jax.sharding import PartitionSpec as P

LOG2E = 1.4426950408889634
HBM = pl.BlockSpec(memory_space=pltpu.HBM)
VMEM = pl.BlockSpec(memory_space=pltpu.VMEM)
SMEM = pl.BlockSpec(memory_space=pltpu.SMEM)


def swap(value, axis, size, bit):
    return lax.ppermute(value, axis, [(i, i ^ bit) for i in range(size)])


def group(here, panel, same, other):
    feats = same.shape[0]
    panel[pl.ds(pl.multiple_of(here[1] * feats, feats), feats), :] = same[...]
    panel[pl.ds(pl.multiple_of((1 - here[1]) * feats, feats), feats), :] = other[...]
    return panel[...].T


def prepare_kernel(here, own, own_rows, rates, other, *refs, width):
    groups, rows = refs[:4], refs[4:7]
    lhs, squares, ordered, half_ref, scale, panel, own_block, rows0, rate, sems = refs[7:]
    copies = [
        pltpu.make_async_copy(own, own_block, sems.at[0]),
        pltpu.make_async_copy(own_rows, rows0, sems.at[1]),
        pltpu.make_async_copy(rates, rate, sems.at[2]),
    ]
    for copy in copies:
        copy.start()
    total = 0.0
    pairs = [(own_block, other), groups[0:2], groups[2:4]]
    for k in (1, 2, 0):
        if k == 0:
            copies[0].wait()
        piece = group(here, panel.at[k], *pairs[k])
        lhs[:, 128 * k : 128 * (k + 1)] = piece
        total += jnp.square(piece.astype(jnp.float32))
    squares[...] = total
    copies[1].wait()
    copies[2].wait()
    n = rows0.shape[0]
    slots = [rows0, *rows]
    step = 256
    for j in range(0, n, step):
        block = slice(j, j + step)
        total = 0.0
        for t in range(4):
            piece = slots[t][block, :]
            k = here[0] ^ t
            ordered[k, block, :] = piece
            total += jnp.square(piece.astype(jnp.float32))
        half_ref[:, block] = 0.5 * jnp.sum(total.T, axis=0, keepdims=True)
    scale[...] = rate[...] * (2.0 * LOG2E / width)


def finish_kernel(here, lhs, squares, ordered, half_ref, scale, same, other, out, panel, last, half_sq, result, sems, *, cols, tile):
    m, n = result.shape
    piece = group(here, panel, same, other)
    last[...] = piece
    total = squares[...] + jnp.square(piece.astype(jnp.float32))
    half_sq[...] = jnp.broadcast_to(0.5 * jnp.sum(total, axis=1, keepdims=True), half_sq.shape)
    sends = []
    for j in range(0, n, cols):
        block = slice(j, j + cols)
        rhs = jnp.concatenate([ordered[k, block, :] for k in range(4)], axis=1)
        for i in range(0, m, tile):
            part = slice(i, i + tile)
            gram = lax.dot_general(
                jnp.concatenate([lhs[part, :], last[part, :]], axis=1),
                rhs,
                (((1,), (1,)), ((), ())),
                preferred_element_type=jnp.float32,
            )
            half_cand = jnp.concatenate([half_sq[part, :]] * (cols // 128), axis=1)
            result[part, block] = jnp.exp2(
                (gram - half_cand - half_ref[:, block]) * scale[:, block]
            )
        sends.append(
            pltpu.make_async_copy(result.at[:, block], out.at[:, block], sems.at[j // cols])
        )
        sends[-1].start()
    for send in sends:
        send.wait()


def prepare(here, own, references, rates, other, groups, rows):
    feats, m = own.shape
    n = references.shape[0]
    stay = [
        pltpu.with_memory_space_constraint(v, pltpu.HBM)
        for v in (own, references, rates.reshape(1, n))
    ]
    return pl.pallas_call(
        functools.partial(prepare_kernel, width=8 * feats),
        in_specs=[SMEM] + [HBM] * 3 + [VMEM] * 8,
        out_specs=[VMEM] * 5,
        out_shape=[
            jax.ShapeDtypeStruct((m, 384), jnp.bfloat16),
            jax.ShapeDtypeStruct((m, 128), jnp.float32),
            jax.ShapeDtypeStruct((4, n, 128), jnp.bfloat16),
            jax.ShapeDtypeStruct((1, n), jnp.float32),
            jax.ShapeDtypeStruct((1, n), jnp.float32),
        ],
        scratch_shapes=[
            pltpu.VMEM((3, 128, m), jnp.bfloat16),
            pltpu.VMEM((feats, m), jnp.bfloat16),
            pltpu.VMEM(references.shape, jnp.bfloat16),
            pltpu.VMEM((1, n), jnp.float32),
            pltpu.SemaphoreType.DMA((3,)),
        ],
        compiler_params=pltpu.CompilerParams(vmem_limit_bytes=24 * 2**20),
        name="prepare",
    )(here, *stay, other, *groups, *rows)


def finish(here, prepared, same, other, cols=256, tile=256):
    m, n = prepared[0].shape[0], prepared[2].shape[1]
    return pl.pallas_call(
        functools.partial(finish_kernel, cols=cols, tile=tile),
        in_specs=[SMEM] + [VMEM] * 7,
        out_specs=HBM,
        out_shape=jax.ShapeDtypeStruct((m, n), jnp.float32),
        scratch_shapes=[
            pltpu.VMEM((128, m), jnp.bfloat16),
            pltpu.VMEM((m, 128), jnp.bfloat16),
            pltpu.VMEM((m, 128), jnp.float32),
            pltpu.VMEM((m, n), jnp.float32),
            pltpu.SemaphoreType.DMA((n // cols,)),
        ],
        compiler_params=pltpu.CompilerParams(vmem_limit_bytes=40 * 2**20),
        name="finish",
    )(here, *prepared, same, other)


def per_device(candidates, references, rates, *, n_row, n_col, n_depth):
    own = candidates.T
    two = swap(own, "col", n_col, 2)
    far = swap(references, "row", n_row, 2)
    one = swap(own, "col", n_col, 1)
    across = [swap(own, "depth", n_depth, 1)]
    two, one = lax.optimization_barrier((two, one))
    three = swap(two, "col", n_col, 1)
    across += [swap(block, "depth", n_depth, 1) for block in (one, two)]
    far, three, across[0], across[1], across[2] = lax.optimization_barrier(
        (far, three, across[0], across[1], across[2])
    )
    across.append(swap(three, "depth", n_depth, 1))
    side = swap(references, "row", n_row, 1)
    farside = swap(far, "row", n_row, 1)
    here = jnp.stack(
        [lax.axis_index("row") ^ lax.axis_index("col"), lax.axis_index("depth")]
    ).astype(jnp.int32)
    prepared = prepare(
        here, own, references, rates, across[0], (one, across[1], two, across[2]), (side, far, farside)
    )
    return finish(here, prepared, three, across[3])


def gathered(candidates, references, rates):
    panel = lax.all_gather(candidates, ("col", "depth"), axis=1, tiled=True)
    whole = lax.all_gather(references, "row", axis=1, tiled=True)
    gram = lax.dot_general(
        panel, whole, (((1,), (1,)), ((), ())), preferred_element_type=jnp.float32
    )
    cand_sq = jnp.sum(jnp.square(panel.astype(jnp.float32)), axis=1)
    ref_sq = jnp.sum(jnp.square(whole.astype(jnp.float32)), axis=1)
    distance = cand_sq[:, None] + ref_sq[None, :] - 2.0 * gram
    return jnp.exp(-rates[None, :] * distance / panel.shape[1])


def solution(mesh):
    sizes = mesh.shape
    placed = (P("row", ("col", "depth")), P(("col", "depth"), "row"), P(("col", "depth")))
    shape = {"n_row": sizes["row"], "n_col": sizes["col"], "n_depth": sizes["depth"]}

    def body(candidates, references, rates):
        if tuple(shape.values()) == (4, 4, 2) and references.shape[1] == 128:
            return per_device(candidates, references, rates, **shape)
        return gathered(candidates, references, rates)

    return jax.shard_map(
        body,
        mesh=mesh,
        in_specs=placed,
        out_specs=P("row", ("col", "depth")),
        check_vma=False,
    )
```

```python
import functools

import jax
import jax.numpy as jnp
from jax import lax
from jax.experimental import pallas as pl
from jax.experimental.pallas import tpu as pltpu
from jax.sharding import PartitionSpec as P

LOG2E = 1.4426950408889634
HBM = pl.BlockSpec(memory_space=pltpu.HBM)
VMEM = pl.BlockSpec(memory_space=pltpu.VMEM)
SMEM = pl.BlockSpec(memory_space=pltpu.SMEM)


def swap(value, axis, size, bit):
    return lax.ppermute(value, axis, [(i, i ^ bit) for i in range(size)])


def group(depth, panel, same, other):
    feats = same.shape[0]
    panel[pl.ds(pl.multiple_of(depth * feats, feats), feats), :] = same[...]
    panel[pl.ds(pl.multiple_of((1 - depth) * feats, feats), feats), :] = other[...]
    return panel[...].T


def square_sums(rows):
    total = sum(jnp.square(r.astype(jnp.float32)) for r in rows)
    return 0.5 * jnp.sum(total.T, axis=0, keepdims=True)


def prepare_kernel(here, own, own_rows, rates, other, *refs, width, step):
    groups, rows = refs[:4], refs[4:6]
    lhs, squares, rows0, half_ref, scale, panel, own_block, rate, sems = refs[6:]
    copies = [
        pltpu.make_async_copy(own, own_block, sems.at[0]),
        pltpu.make_async_copy(own_rows, rows0, sems.at[1]),
        pltpu.make_async_copy(rates, rate, sems.at[2]),
    ]
    for copy in copies:
        copy.start()
    total = 0.0
    pairs = [(own_block, other), groups[0:2], groups[2:4]]
    for k in (1, 2, 0):
        if k == 0:
            copies[0].wait()
        piece = group(here[1], panel.at[k], *pairs[k])
        lhs[here[0] ^ k] = piece
        total += jnp.square(piece.astype(jnp.float32))
    squares[...] = total
    copies[1].wait()
    copies[2].wait()
    for j in range(0, rows0.shape[0], step):
        block = slice(j, j + step)
        half_ref[:, block] = square_sums([r[block, :] for r in (rows0, *rows)])
    scale[...] = rate[...] * (2.0 * LOG2E / width)


def finish_kernel(
    here, lhs, squares, rows0, half_ref, scale, side, far, farside, same, other, out,
    panel, whole, half_sq, result, sems, *, cols, tile,
):
    m, n = result.shape
    for t in range(4):
        whole[t] = lhs[t]
    piece = group(here[1], panel, same, other)
    whole[here[0] ^ 3] = piece
    total = squares[...] + jnp.square(piece.astype(jnp.float32))
    half_sq[...] = jnp.broadcast_to(0.5 * jnp.sum(total, axis=1, keepdims=True), half_sq.shape)
    sends = []
    for j in range(0, n, cols):
        block = slice(j, j + cols)
        rhs = jnp.concatenate([r[block, :] for r in (rows0, side, far, farside)], axis=1)
        half = half_ref[:, block] + square_sums([farside[block, :]])
        for i in range(0, m, tile):
            part = slice(i, i + tile)
            gram = lax.dot_general(
                jnp.concatenate([whole[t, part, :] for t in range(4)], axis=1),
                rhs,
                (((1,), (1,)), ((), ())),
                preferred_element_type=jnp.float32,
            )
            half_cand = jnp.concatenate([half_sq[part, :]] * (cols // 128), axis=1)
            result[part, block] = jnp.exp2((gram - half_cand - half) * scale[:, block])
        sends.append(
            pltpu.make_async_copy(result.at[:, block], out.at[:, block], sems.at[j // cols])
        )
        sends[-1].start()
    for send in sends:
        send.wait()


def prepare(here, own, references, rates, other, groups, rows):
    feats, m = own.shape
    n = references.shape[0]
    stay = [
        pltpu.with_memory_space_constraint(v, pltpu.HBM)
        for v in (own, references, rates.reshape(1, n))
    ]
    return pl.pallas_call(
        functools.partial(prepare_kernel, width=8 * feats, step=256),
        in_specs=[SMEM] + [HBM] * 3 + [VMEM] * 7,
        out_specs=[VMEM] * 5,
        out_shape=[
            jax.ShapeDtypeStruct((4, m, 128), jnp.bfloat16),
            jax.ShapeDtypeStruct((m, 128), jnp.float32),
            jax.ShapeDtypeStruct(references.shape, jnp.bfloat16),
            jax.ShapeDtypeStruct((1, n), jnp.float32),
            jax.ShapeDtypeStruct((1, n), jnp.float32),
        ],
        scratch_shapes=[
            pltpu.VMEM((3, 128, m), jnp.bfloat16),
            pltpu.VMEM((feats, m), jnp.bfloat16),
            pltpu.VMEM((1, n), jnp.float32),
            pltpu.SemaphoreType.DMA((3,)),
        ],
        compiler_params=pltpu.CompilerParams(vmem_limit_bytes=24 * 2**20),
        name="prepare",
    )(here, *stay, other, *groups, *rows)


def finish(here, prepared, rows, same, other, cols=256, tile=256):
    m, n = prepared[1].shape[0], prepared[2].shape[0]
    return pl.pallas_call(
        functools.partial(finish_kernel, cols=cols, tile=tile),
        in_specs=[SMEM] + [VMEM] * 10,
        out_specs=HBM,
        out_shape=jax.ShapeDtypeStruct((m, n), jnp.float32),
        scratch_shapes=[
            pltpu.VMEM((128, m), jnp.bfloat16),
            pltpu.VMEM((4, m, 128), jnp.bfloat16),
            pltpu.VMEM((m, 128), jnp.float32),
            pltpu.VMEM((m, n), jnp.float32),
            pltpu.SemaphoreType.DMA((n // cols,)),
        ],
        compiler_params=pltpu.CompilerParams(vmem_limit_bytes=40 * 2**20),
        name="finish",
    )(here, *prepared, *rows, same, other)


def per_device(candidates, references, rates, *, n_row, n_col, n_depth):
    own = candidates.T
    far = swap(references, "row", n_row, 2)
    two = swap(own, "col", n_col, 2)
    side = swap(references, "row", n_row, 1)
    late, side = lax.optimization_barrier((own, side))
    one = swap(late, "col", n_col, 1)
    y0 = swap(late, "depth", n_depth, 1)
    y3 = lax.ppermute(late, ("col", "depth"), [(i, i ^ 7) for i in range(8)])
    two, one = lax.optimization_barrier((two, one))
    three = swap(two, "col", n_col, 1)
    y1 = swap(one, "depth", n_depth, 1)
    y2 = swap(two, "depth", n_depth, 1)
    far, y0, y1, y2, three, y3 = lax.optimization_barrier((far, y0, y1, y2, three, y3))
    farside = swap(far, "row", n_row, 1)
    across = [y0, y1, y2, y3]
    here = jnp.stack(
        [lax.axis_index("row") ^ lax.axis_index("col"), lax.axis_index("depth")]
    ).astype(jnp.int32)
    prepared = prepare(
        here, own, references, rates, across[0], (one, across[1], two, across[2]), (side, far)
    )
    return finish(here, prepared, (side, far, farside), three, across[3])


def gathered(candidates, references, rates):
    panel = lax.all_gather(candidates, ("col", "depth"), axis=1, tiled=True)
    whole = lax.all_gather(references, "row", axis=1, tiled=True)
    gram = lax.dot_general(
        panel, whole, (((1,), (1,)), ((), ())), preferred_element_type=jnp.float32
    )
    cand_sq = jnp.sum(jnp.square(panel.astype(jnp.float32)), axis=1)
    ref_sq = jnp.sum(jnp.square(whole.astype(jnp.float32)), axis=1)
    distance = cand_sq[:, None] + ref_sq[None, :] - 2.0 * gram
    return jnp.exp(-rates[None, :] * distance / panel.shape[1])


def solution(mesh):
    sizes = mesh.shape
    placed = (P("row", ("col", "depth")), P(("col", "depth"), "row"), P(("col", "depth")))
    shape = {"n_row": sizes["row"], "n_col": sizes["col"], "n_depth": sizes["depth"]}

    def body(candidates, references, rates):
        if tuple(shape.values()) == (4, 4, 2) and references.shape[1] == 128:
            return per_device(candidates, references, rates, **shape)
        return gathered(candidates, references, rates)

    return jax.shard_map(
        body,
        mesh=mesh,
        in_specs=placed,
        out_specs=P("row", ("col", "depth")),
        check_vma=False,
    )
```

```python
import functools

import jax
import jax.numpy as jnp
from jax import lax
from jax.experimental import pallas as pl
from jax.experimental.pallas import tpu as pltpu
from jax.sharding import PartitionSpec as P

LOG2E = 1.4426950408889634
HBM = pl.BlockSpec(memory_space=pltpu.HBM)
VMEM = pl.BlockSpec(memory_space=pltpu.VMEM)
SMEM = pl.BlockSpec(memory_space=pltpu.SMEM)


def swap(value, axis, size, bit):
    return lax.ppermute(value, axis, [(i, i ^ bit) for i in range(size)])


def group(depth, panel, same, other):
    feats = same.shape[0]
    panel[pl.ds(pl.multiple_of(depth * feats, feats), feats), :] = same[...]
    panel[pl.ds(pl.multiple_of((1 - depth) * feats, feats), feats), :] = other[...]
    return panel[...].T


def square_sums(rows):
    total = sum(jnp.square(r.astype(jnp.float32)) for r in rows)
    return 0.5 * jnp.sum(total.T, axis=0, keepdims=True)


def prepare_kernel(here, own, own_rows, rates, other, *refs, width, step):
    groups, rows = refs[:4], refs[4:6]
    lhs, squares, rows0, half_ref, scale, panel, own_block, rate, sems = refs[6:]
    copies = [
        pltpu.make_async_copy(own, own_block, sems.at[0]),
        pltpu.make_async_copy(own_rows, rows0, sems.at[1]),
        pltpu.make_async_copy(rates, rate, sems.at[2]),
    ]
    for copy in copies:
        copy.start()
    total = 0.0
    pairs = [(own_block, other), groups[0:2], groups[2:4]]
    step_of = (0, 1, 3)
    for k in (1, 2, 0):
        if k == 0:
            copies[0].wait()
        piece = group(here[1], panel.at[k], *pairs[k])
        lhs[here[0] ^ step_of[k]] = piece
        total += jnp.square(piece.astype(jnp.float32))
    squares[...] = total
    copies[1].wait()
    copies[2].wait()
    for j in range(0, rows0.shape[0], step):
        block = slice(j, j + step)
        half_ref[:, block] = square_sums([r[block, :] for r in (rows0, *rows)])
    scale[...] = rate[...] * (2.0 * LOG2E / width)


def turn_kernel(here, squares, same, other, turned, half_sq, panel):
    piece = group(here[1], panel, same, other)
    turned[...] = piece
    total = squares[...] + jnp.square(piece.astype(jnp.float32))
    half_sq[...] = jnp.broadcast_to(0.5 * jnp.sum(total, axis=1, keepdims=True), half_sq.shape)


def finish_kernel(
    here, lhs, rows0, half_ref, scale, side, far, farside, turned, half_sq, out,
    whole, result, sems, *, cols, tile,
):
    m, n = result.shape
    for t in range(4):
        whole[t] = lhs[t]
    whole[here[0] ^ 2] = turned[...]
    sends = []
    for j in range(0, n, cols):
        block = slice(j, j + cols)
        rhs = jnp.concatenate([r[block, :] for r in (rows0, side, far, farside)], axis=1)
        half = half_ref[:, block] + square_sums([farside[block, :]])
        for i in range(0, m, tile):
            part = slice(i, i + tile)
            gram = lax.dot_general(
                jnp.concatenate([whole[t, part, :] for t in range(4)], axis=1),
                rhs,
                (((1,), (1,)), ((), ())),
                preferred_element_type=jnp.float32,
            )
            half_cand = jnp.concatenate([half_sq[part, :]] * (cols // 128), axis=1)
            result[part, block] = jnp.exp2((gram - half_cand - half) * scale[:, block])
        sends.append(
            pltpu.make_async_copy(result.at[:, block], out.at[:, block], sems.at[j // cols])
        )
        sends[-1].start()
    for send in sends:
        send.wait()


def prepare(here, own, references, rates, other, groups, rows):
    feats, m = own.shape
    n = references.shape[0]
    stay = [
        pltpu.with_memory_space_constraint(v, pltpu.HBM)
        for v in (own, references, rates.reshape(1, n))
    ]
    return pl.pallas_call(
        functools.partial(prepare_kernel, width=8 * feats, step=256),
        in_specs=[SMEM] + [HBM] * 3 + [VMEM] * 7,
        out_specs=[VMEM] * 5,
        out_shape=[
            jax.ShapeDtypeStruct((4, m, 128), jnp.bfloat16),
            jax.ShapeDtypeStruct((m, 128), jnp.float32),
            jax.ShapeDtypeStruct(references.shape, jnp.bfloat16),
            jax.ShapeDtypeStruct((1, n), jnp.float32),
            jax.ShapeDtypeStruct((1, n), jnp.float32),
        ],
        scratch_shapes=[
            pltpu.VMEM((3, 128, m), jnp.bfloat16),
            pltpu.VMEM((feats, m), jnp.bfloat16),
            pltpu.VMEM((1, n), jnp.float32),
            pltpu.SemaphoreType.DMA((3,)),
        ],
        compiler_params=pltpu.CompilerParams(vmem_limit_bytes=24 * 2**20),
        name="prepare",
    )(here, *stay, other, *groups, *rows)


def turn(here, squares, same, other):
    m = squares.shape[0]
    return pl.pallas_call(
        turn_kernel,
        in_specs=[SMEM] + [VMEM] * 3,
        out_specs=[VMEM] * 2,
        out_shape=[
            jax.ShapeDtypeStruct((m, 128), jnp.bfloat16),
            jax.ShapeDtypeStruct((m, 128), jnp.float32),
        ],
        scratch_shapes=[pltpu.VMEM((128, m), jnp.bfloat16)],
        compiler_params=pltpu.CompilerParams(vmem_limit_bytes=8 * 2**20),
        cost_estimate=pl.CostEstimate(flops=10000000000, bytes_accessed=4194304, transcendentals=0),
        name="turn",
    )(here, squares, same, other)


def finish(here, prepared, rows, turned, cols=256, tile=256):
    m, n = prepared[0].shape[1], prepared[1].shape[0]
    return pl.pallas_call(
        functools.partial(finish_kernel, cols=cols, tile=tile),
        in_specs=[SMEM] + [VMEM] * 9,
        out_specs=HBM,
        out_shape=jax.ShapeDtypeStruct((m, n), jnp.float32),
        scratch_shapes=[
            pltpu.VMEM((4, m, 128), jnp.bfloat16),
            pltpu.VMEM((m, n), jnp.float32),
            pltpu.SemaphoreType.DMA((n // cols,)),
        ],
        compiler_params=pltpu.CompilerParams(vmem_limit_bytes=40 * 2**20),
        name="finish",
    )(here, *prepared, *rows, *turned)


def per_device(candidates, references, rates, *, n_row, n_col, n_depth):
    own = candidates.T
    far = swap(references, "row", n_row, 2)
    two = swap(own, "col", n_col, 2)
    side = swap(references, "row", n_row, 1)
    late, side = lax.optimization_barrier((own, side))
    one = swap(late, "col", n_col, 1)
    y0 = swap(late, "depth", n_depth, 1)
    y3 = lax.ppermute(late, ("col", "depth"), [(i, i ^ 7) for i in range(8)])
    two, one = lax.optimization_barrier((two, one))
    three = swap(two, "col", n_col, 1)
    y1 = swap(one, "depth", n_depth, 1)
    y2 = swap(two, "depth", n_depth, 1)
    far, y0, y3 = lax.optimization_barrier((far, y0, y3))
    farside = swap(far, "row", n_row, 1)
    y1, three = lax.optimization_barrier((y1, three))
    here = jnp.stack(
        [lax.axis_index("row") ^ lax.axis_index("col"), lax.axis_index("depth")]
    ).astype(jnp.int32)
    lhs, squares, *prepared = prepare(
        here, own, references, rates, y0, (one, y1, three, y3), (side, far)
    )
    turned = turn(here, squares, two, y2)
    return finish(here, (lhs, *prepared), (side, far, farside), turned)


def gathered(candidates, references, rates):
    panel = lax.all_gather(candidates, ("col", "depth"), axis=1, tiled=True)
    whole = lax.all_gather(references, "row", axis=1, tiled=True)
    gram = lax.dot_general(
        panel, whole, (((1,), (1,)), ((), ())), preferred_element_type=jnp.float32
    )
    cand_sq = jnp.sum(jnp.square(panel.astype(jnp.float32)), axis=1)
    ref_sq = jnp.sum(jnp.square(whole.astype(jnp.float32)), axis=1)
    distance = cand_sq[:, None] + ref_sq[None, :] - 2.0 * gram
    return jnp.exp(-rates[None, :] * distance / panel.shape[1])


def solution(mesh):
    sizes = mesh.shape
    placed = (P("row", ("col", "depth")), P(("col", "depth"), "row"), P(("col", "depth")))
    shape = {"n_row": sizes["row"], "n_col": sizes["col"], "n_depth": sizes["depth"]}

    def body(candidates, references, rates):
        if tuple(shape.values()) == (4, 4, 2) and references.shape[1] == 128:
            return per_device(candidates, references, rates, **shape)
        return gathered(candidates, references, rates)

    return jax.shard_map(
        body,
        mesh=mesh,
        in_specs=placed,
        out_specs=P("row", ("col", "depth")),
        check_vma=False,
    )
```

```python
import functools

import jax
import jax.numpy as jnp
from jax import lax
from jax.experimental import pallas as pl
from jax.experimental.pallas import tpu as pltpu
from jax.sharding import PartitionSpec as P

LOG2E = 1.4426950408889634
HBM = pl.BlockSpec(memory_space=pltpu.HBM)
VMEM = pl.BlockSpec(memory_space=pltpu.VMEM)
SMEM = pl.BlockSpec(memory_space=pltpu.SMEM)


def swap(value, axis, size, bit):
    return lax.ppermute(value, axis, [(i, i ^ bit) for i in range(size)])


def group(depth, panel, same, other):
    feats = same.shape[0]
    panel[pl.ds(pl.multiple_of(depth * feats, feats), feats), :] = same[...]
    panel[pl.ds(pl.multiple_of((1 - depth) * feats, feats), feats), :] = other[...]
    return panel[...].T


def square_sums(rows):
    total = sum(jnp.square(r.astype(jnp.float32)) for r in rows)
    return 0.5 * jnp.sum(total.T, axis=0, keepdims=True)


def prepare_kernel(here, own, own_rows, rates, other, *refs, width, step):
    groups, rows = refs[:4], refs[4:6]
    lhs, squares, rows0, half_ref, scale, panel, own_block, rate, sems = refs[6:]
    copies = [
        pltpu.make_async_copy(own, own_block, sems.at[0]),
        pltpu.make_async_copy(own_rows, rows0, sems.at[1]),
        pltpu.make_async_copy(rates, rate, sems.at[2]),
    ]
    for copy in copies:
        copy.start()
    total = 0.0
    pairs = [(own_block, other), groups[0:2], groups[2:4]]
    step_of = (0, 1, 3)
    for k in (1, 2, 0):
        if k == 0:
            copies[0].wait()
        piece = group(here[1], panel.at[k], *pairs[k])
        lhs[here[0] ^ step_of[k]] = piece
        total += jnp.square(piece.astype(jnp.float32))
    squares[...] = total
    copies[1].wait()
    copies[2].wait()
    for j in range(0, rows0.shape[0], step):
        block = slice(j, j + step)
        half_ref[:, block] = square_sums([r[block, :] for r in (rows0, *rows)])
    scale[...] = rate[...] * (2.0 * LOG2E / width)


def turn_kernel(here, squares, same, other, turned, half_sq, panel):
    piece = group(here[1], panel, same, other)
    turned[...] = piece
    half_sq[...] = squares[...] + jnp.square(piece.astype(jnp.float32))


def finish_kernel(
    here, lhs, rows0, half_ref, scale, side, far, farside, turned, squares, out,
    whole, half_sq, result, sems, *, cols, tile,
):
    m, n = result.shape
    for t in range(4):
        whole[t] = lhs[t]
    whole[here[0] ^ 2] = turned[...]
    half_sq[...] = jnp.broadcast_to(
        0.5 * jnp.sum(squares[...], axis=1, keepdims=True), half_sq.shape
    )
    sends = []
    for j in range(0, n, cols):
        block = slice(j, j + cols)
        rhs = jnp.concatenate([r[block, :] for r in (rows0, side, far, farside)], axis=1)
        half = half_ref[:, block] + square_sums([farside[block, :]])
        for i in range(0, m, tile):
            part = slice(i, i + tile)
            gram = lax.dot_general(
                jnp.concatenate([whole[t, part, :] for t in range(4)], axis=1),
                rhs,
                (((1,), (1,)), ((), ())),
                preferred_element_type=jnp.float32,
            )
            half_cand = jnp.concatenate([half_sq[part, :]] * (cols // 128), axis=1)
            result[part, block] = jnp.exp2((gram - half_cand - half) * scale[:, block])
        sends.append(
            pltpu.make_async_copy(result.at[:, block], out.at[:, block], sems.at[j // cols])
        )
        sends[-1].start()
    for send in sends:
        send.wait()


def prepare(here, own, references, rates, other, groups, rows):
    feats, m = own.shape
    n = references.shape[0]
    stay = [
        pltpu.with_memory_space_constraint(v, pltpu.HBM)
        for v in (own, references, rates.reshape(1, n))
    ]
    return pl.pallas_call(
        functools.partial(prepare_kernel, width=8 * feats, step=256),
        in_specs=[SMEM] + [HBM] * 3 + [VMEM] * 7,
        out_specs=[VMEM] * 5,
        out_shape=[
            jax.ShapeDtypeStruct((4, m, 128), jnp.bfloat16),
            jax.ShapeDtypeStruct((m, 128), jnp.float32),
            jax.ShapeDtypeStruct(references.shape, jnp.bfloat16),
            jax.ShapeDtypeStruct((1, n), jnp.float32),
            jax.ShapeDtypeStruct((1, n), jnp.float32),
        ],
        scratch_shapes=[
            pltpu.VMEM((3, 128, m), jnp.bfloat16),
            pltpu.VMEM((feats, m), jnp.bfloat16),
            pltpu.VMEM((1, n), jnp.float32),
            pltpu.SemaphoreType.DMA((3,)),
        ],
        compiler_params=pltpu.CompilerParams(vmem_limit_bytes=24 * 2**20),
        name="prepare",
    )(here, *stay, other, *groups, *rows)


def turn(here, squares, same, other):
    m = squares.shape[0]
    return pl.pallas_call(
        turn_kernel,
        in_specs=[SMEM] + [VMEM] * 3,
        out_specs=[VMEM] * 2,
        out_shape=[
            jax.ShapeDtypeStruct((m, 128), jnp.bfloat16),
            jax.ShapeDtypeStruct((m, 128), jnp.float32),
        ],
        scratch_shapes=[pltpu.VMEM((128, m), jnp.bfloat16)],
        compiler_params=pltpu.CompilerParams(vmem_limit_bytes=8 * 2**20),
        cost_estimate=pl.CostEstimate(flops=10000000000, bytes_accessed=4194304, transcendentals=0),
        name="turn",
    )(here, squares, same, other)


def finish(here, prepared, rows, turned, cols=256, tile=256):
    m, n = prepared[0].shape[1], prepared[1].shape[0]
    return pl.pallas_call(
        functools.partial(finish_kernel, cols=cols, tile=tile),
        in_specs=[SMEM] + [VMEM] * 9,
        out_specs=HBM,
        out_shape=jax.ShapeDtypeStruct((m, n), jnp.float32),
        scratch_shapes=[
            pltpu.VMEM((4, m, 128), jnp.bfloat16),
            pltpu.VMEM((m, 128), jnp.float32),
            pltpu.VMEM((m, n), jnp.float32),
            pltpu.SemaphoreType.DMA((n // cols,)),
        ],
        compiler_params=pltpu.CompilerParams(vmem_limit_bytes=40 * 2**20),
        name="finish",
    )(here, *prepared, *rows, *turned)


def per_device(candidates, references, rates, *, n_row, n_col, n_depth):
    own = candidates.T
    far = swap(references, "row", n_row, 2)
    two = swap(own, "col", n_col, 2)
    side = swap(references, "row", n_row, 1)
    late, side = lax.optimization_barrier((own, side))
    one = swap(late, "col", n_col, 1)
    y0 = swap(late, "depth", n_depth, 1)
    y3 = lax.ppermute(late, ("col", "depth"), [(i, i ^ 7) for i in range(8)])
    two, one = lax.optimization_barrier((two, one))
    three = swap(two, "col", n_col, 1)
    y1 = swap(one, "depth", n_depth, 1)
    y2 = swap(two, "depth", n_depth, 1)
    far, y0, y3 = lax.optimization_barrier((far, y0, y3))
    farside = swap(far, "row", n_row, 1)
    y1, three = lax.optimization_barrier((y1, three))
    here = jnp.stack(
        [lax.axis_index("row") ^ lax.axis_index("col"), lax.axis_index("depth")]
    ).astype(jnp.int32)
    lhs, squares, *prepared = prepare(
        here, own, references, rates, y0, (one, y1, three, y3), (side, far)
    )
    turned = turn(here, squares, two, y2)
    return finish(here, (lhs, *prepared), (side, far, farside), turned)


def gathered(candidates, references, rates):
    panel = lax.all_gather(candidates, ("col", "depth"), axis=1, tiled=True)
    whole = lax.all_gather(references, "row", axis=1, tiled=True)
    gram = lax.dot_general(
        panel, whole, (((1,), (1,)), ((), ())), preferred_element_type=jnp.float32
    )
    cand_sq = jnp.sum(jnp.square(panel.astype(jnp.float32)), axis=1)
    ref_sq = jnp.sum(jnp.square(whole.astype(jnp.float32)), axis=1)
    distance = cand_sq[:, None] + ref_sq[None, :] - 2.0 * gram
    return jnp.exp(-rates[None, :] * distance / panel.shape[1])


def solution(mesh):
    sizes = mesh.shape
    placed = (P("row", ("col", "depth")), P(("col", "depth"), "row"), P(("col", "depth")))
    shape = {"n_row": sizes["row"], "n_col": sizes["col"], "n_depth": sizes["depth"]}

    def body(candidates, references, rates):
        if tuple(shape.values()) == (4, 4, 2) and references.shape[1] == 128:
            return per_device(candidates, references, rates, **shape)
        return gathered(candidates, references, rates)

    return jax.shard_map(
        body,
        mesh=mesh,
        in_specs=placed,
        out_specs=P("row", ("col", "depth")),
        check_vma=False,
    )
```

```python
import functools

import jax
import jax.numpy as jnp
from jax import lax
from jax.experimental import pallas as pl
from jax.experimental.pallas import tpu as pltpu
from jax.sharding import PartitionSpec as P

LOG2E = 1.4426950408889634
HBM = pl.BlockSpec(memory_space=pltpu.HBM)
VMEM = pl.BlockSpec(memory_space=pltpu.VMEM)
SMEM = pl.BlockSpec(memory_space=pltpu.SMEM)


def swap(value, axis, size, bit):
    return lax.ppermute(value, axis, [(i, i ^ bit) for i in range(size)])


def group(depth, panel, same, other):
    feats = same.shape[0]
    panel[pl.ds(pl.multiple_of(depth * feats, feats), feats), :] = same[...]
    panel[pl.ds(pl.multiple_of((1 - depth) * feats, feats), feats), :] = other[...]
    return panel[...].T


def square_sums(rows):
    total = sum(jnp.square(r.astype(jnp.float32)) for r in rows)
    return 0.5 * jnp.sum(total.T, axis=0, keepdims=True)


def prepare_kernel(here, own, own_rows, rates, other, *refs, width, step):
    groups, rows = refs[:4], refs[4:6]
    lhs, squares, rows0, half_ref, scale, panel, own_block, rate, sems = refs[6:]
    copies = [
        pltpu.make_async_copy(own, own_block, sems.at[0]),
        pltpu.make_async_copy(own_rows, rows0, sems.at[1]),
        pltpu.make_async_copy(rates, rate, sems.at[2]),
    ]
    for copy in copies:
        copy.start()
    total = 0.0
    pairs = [(own_block, other), groups[0:2], groups[2:4]]
    step_of = (0, 1, 3)
    for k in (1, 2, 0):
        if k == 0:
            copies[0].wait()
        piece = group(here[1], panel.at[k], *pairs[k])
        lhs[here[0] ^ step_of[k]] = piece
        total += jnp.square(piece.astype(jnp.float32))
    squares[...] = total
    copies[1].wait()
    copies[2].wait()
    for j in range(0, rows0.shape[0], step):
        block = slice(j, j + step)
        half_ref[:, block] = square_sums([r[block, :] for r in (rows0, *rows)])
    scale[...] = rate[...] * (2.0 * LOG2E / width)


def turn_kernel(here, squares, same, other, turned, half_sq, panel):
    piece = group(here[1], panel, same, other)
    turned[...] = piece
    half_sq[...] = squares[...] + jnp.square(piece.astype(jnp.float32))


def finish_kernel(
    here, lhs, rows0, half_ref, scale, side, far, farside, turned, squares, out,
    whole, half_sq, result, sems, *, cols, tile,
):
    m, n = result.shape
    for t in range(4):
        whole[t] = lhs[t]
    whole[here[0] ^ 2] = turned[...]
    half_sq[...] = jnp.broadcast_to(
        0.5 * jnp.sum(squares[...], axis=1, keepdims=True), half_sq.shape
    )
    sends = []
    for j in range(0, n, cols):
        block = slice(j, j + cols)
        rhs = jnp.concatenate([r[block, :] for r in (rows0, side, far, farside)], axis=1)
        half = half_ref[:, block] + square_sums([farside[block, :]])
        for i in range(0, m, tile):
            part = slice(i, i + tile)
            gram = lax.dot_general(
                jnp.concatenate([whole[t, part, :] for t in range(4)], axis=1),
                rhs,
                (((1,), (1,)), ((), ())),
                preferred_element_type=jnp.float32,
            )
            half_cand = jnp.concatenate([half_sq[part, :]] * (cols // 128), axis=1)
            result[part, block] = jnp.exp2((gram - half_cand - half) * scale[:, block])
        sends.append(
            pltpu.make_async_copy(result.at[:, block], out.at[:, block], sems.at[j // cols])
        )
        sends[-1].start()
    for send in sends:
        send.wait()


def prepare(here, own, references, rates, other, groups, rows):
    feats, m = own.shape
    n = references.shape[0]
    stay = [
        pltpu.with_memory_space_constraint(v, pltpu.HBM)
        for v in (own, references, rates.reshape(1, n))
    ]
    return pl.pallas_call(
        functools.partial(prepare_kernel, width=8 * feats, step=256),
        in_specs=[SMEM] + [HBM] * 3 + [VMEM] * 7,
        out_specs=[VMEM] * 5,
        out_shape=[
            jax.ShapeDtypeStruct((4, m, 128), jnp.bfloat16),
            jax.ShapeDtypeStruct((m, 128), jnp.float32),
            jax.ShapeDtypeStruct(references.shape, jnp.bfloat16),
            jax.ShapeDtypeStruct((1, n), jnp.float32),
            jax.ShapeDtypeStruct((1, n), jnp.float32),
        ],
        scratch_shapes=[
            pltpu.VMEM((3, 128, m), jnp.bfloat16),
            pltpu.VMEM((feats, m), jnp.bfloat16),
            pltpu.VMEM((1, n), jnp.float32),
            pltpu.SemaphoreType.DMA((3,)),
        ],
        compiler_params=pltpu.CompilerParams(vmem_limit_bytes=24 * 2**20),
        name="prepare",
    )(here, *stay, other, *groups, *rows)


def turn(here, squares, same, other):
    m = squares.shape[0]
    return pl.pallas_call(
        turn_kernel,
        in_specs=[SMEM] + [VMEM] * 3,
        out_specs=[VMEM] * 2,
        out_shape=[
            jax.ShapeDtypeStruct((m, 128), jnp.bfloat16),
            jax.ShapeDtypeStruct((m, 128), jnp.float32),
        ],
        scratch_shapes=[pltpu.VMEM((128, m), jnp.bfloat16)],
        compiler_params=pltpu.CompilerParams(vmem_limit_bytes=8 * 2**20),
        cost_estimate=pl.CostEstimate(flops=10000000000, bytes_accessed=4194304, transcendentals=0),
        name="turn",
    )(here, squares, same, other)


def finish(here, prepared, rows, turned, cols=256, tile=256):
    m, n = prepared[0].shape[1], prepared[1].shape[0]
    return pl.pallas_call(
        functools.partial(finish_kernel, cols=cols, tile=tile),
        in_specs=[SMEM] + [VMEM] * 9,
        out_specs=HBM,
        out_shape=jax.ShapeDtypeStruct((m, n), jnp.float32),
        scratch_shapes=[
            pltpu.VMEM((4, m, 128), jnp.bfloat16),
            pltpu.VMEM((m, 128), jnp.float32),
            pltpu.VMEM((m, n), jnp.float32),
            pltpu.SemaphoreType.DMA((n // cols,)),
        ],
        compiler_params=pltpu.CompilerParams(vmem_limit_bytes=40 * 2**20),
        name="finish",
    )(here, *prepared, *rows, *turned)


def per_device(candidates, references, rates, *, n_row, n_col, n_depth):
    own = candidates.T
    far = swap(references, "row", n_row, 2)
    two = swap(own, "col", n_col, 2)
    side = swap(references, "row", n_row, 1)
    late, side = lax.optimization_barrier((own, side))
    one = swap(late, "col", n_col, 1)
    y0 = swap(late, "depth", n_depth, 1)
    y3 = lax.ppermute(late, ("col", "depth"), [(i, i ^ 7) for i in range(8)])
    one, two = lax.optimization_barrier((one, two))
    y1 = swap(one, "depth", n_depth, 1)
    three = swap(two, "col", n_col, 1)
    y2 = swap(two, "depth", n_depth, 1)
    far, y0, y3 = lax.optimization_barrier((far, y0, y3))
    farside = swap(far, "row", n_row, 1)
    y1, three = lax.optimization_barrier((y1, three))
    here = jnp.stack(
        [lax.axis_index("row") ^ lax.axis_index("col"), lax.axis_index("depth")]
    ).astype(jnp.int32)
    lhs, squares, *prepared = prepare(
        here, own, references, rates, y0, (one, y1, three, y3), (side, far)
    )
    turned = turn(here, squares, two, y2)
    return finish(here, (lhs, *prepared), (side, far, farside), turned)


def gathered(candidates, references, rates):
    panel = lax.all_gather(candidates, ("col", "depth"), axis=1, tiled=True)
    whole = lax.all_gather(references, "row", axis=1, tiled=True)
    gram = lax.dot_general(
        panel, whole, (((1,), (1,)), ((), ())), preferred_element_type=jnp.float32
    )
    cand_sq = jnp.sum(jnp.square(panel.astype(jnp.float32)), axis=1)
    ref_sq = jnp.sum(jnp.square(whole.astype(jnp.float32)), axis=1)
    distance = cand_sq[:, None] + ref_sq[None, :] - 2.0 * gram
    return jnp.exp(-rates[None, :] * distance / panel.shape[1])


def solution(mesh):
    sizes = mesh.shape
    placed = (P("row", ("col", "depth")), P(("col", "depth"), "row"), P(("col", "depth")))
    shape = {"n_row": sizes["row"], "n_col": sizes["col"], "n_depth": sizes["depth"]}

    def body(candidates, references, rates):
        if tuple(shape.values()) == (4, 4, 2) and references.shape[1] == 128:
            return per_device(candidates, references, rates, **shape)
        return gathered(candidates, references, rates)

    return jax.shard_map(
        body,
        mesh=mesh,
        in_specs=placed,
        out_specs=P("row", ("col", "depth")),
        check_vma=False,
    )
```
